256 devices in a mesh: row: 32 (over y, x, core), col: 8 (over z).
Axes of the slice: x: 4, y: 4, z: 8, core: 2. Of those that a mesh axis runs over, the one named last changes fastest.
Arguments:
- inputs: bfloat16 [768, 12288], P(None, 'col'), may hold values from -6 to 6
- out_grad: bfloat16 [768, 12288], P(None, 'col'), may hold values from -6 to 6
- pre_act: bfloat16 [768, 24576], P('col', 'row'), may hold values from -8 to 8
- w_in: bfloat16 [12288, 24576], P('col', 'row'), may hold values from -0.0546875 to 0.0546875
- w_out: bfloat16 [24576, 12288], P('row', 'col'), may hold values from -0.0390625 to 0.0390625
Outputs:
- grad_inputs: bfloat16 [768, 12288], P('row', 'col')
- grad_w_in: bfloat16 [12288, 24576], P('col', 'row')
- grad_w_out: bfloat16 [24576, 12288], P('row', 'col')
The draws below stay inside these ranges and needn't reach their ends.
All inputs are finite; a program needn't handle non-finite values.
Results may differ from the reference program's by a relative error of at most 0.0049.
Values may be sent and summed in bfloat16 or wider, within the bound.
A program may use at most 64 MiB of HBM per device.

```python
import math
import jax
import jax.numpy as jnp
from jax import lax

D = 12288
FW = 24576
TOKENS = 768


def level_of(key, shape, shards, smallest, largest):
    def one(dim, blocks):
        draws = jax.random.uniform(jax.random.fold_in(jax.random.fold_in(key, 6), dim), (blocks,), jnp.float32, smallest / len(shards), largest / len(shards))
        return jnp.repeat(jnp.exp(draws), shape[dim] // blocks).reshape((-1,) + (1,) * (len(shape) - dim - 1))

    gain = one(*shards[0])
    for cut in shards[1:]:
        gain = gain * one(*cut)
    return gain


def bell_draw(own_key, extent, width, most, shards=(), kind=jnp.bfloat16):
    array = width * jax.random.normal(own_key, extent, jnp.float32)
    if shards:
        array = array * level_of(own_key, extent, shards, -0.22, 0.18)
    return jnp.clip(array, -most, most).astype(kind)


def setup_inputs(seed: int = 0) -> dict:
    key_list = jax.random.split(jax.random.key(seed), 6)
    inputs = bell_draw(key_list[0], (TOKENS, D), 1.0, 6.0, ((1, 8),))
    out_grad = bell_draw(key_list[1], (TOKENS, D), 1.0, 6.0, ((1, 8),))
    pre_act = bell_draw(key_list[2], (TOKENS, FW), 1.5, 8.0, ((0, 8), (1, 32)))
    w_in = bell_draw(key_list[3], (D, FW), D ** -0.5, 0.0546875, ((0, 8), (1, 32)))
    w_out = bell_draw(key_list[4], (FW, D), FW ** -0.5, 0.0390625, ((0, 32), (1, 8)))
    return dict(inputs=inputs, out_grad=out_grad, pre_act=pre_act, w_in=w_in, w_out=w_out)


coef_c = math.sqrt(2.0 / math.pi)

def gelu_parts(pre_values):
    hval = pre_values.astype(jnp.float32)
    tval = jnp.tanh(coef_c * (hval + 0.044715 * hval * hval * hval))
    activ = 0.5 * hval * (1.0 + tval)
    deriv = 0.5 * (1.0 + tval) + 0.5 * hval * (1.0 - tval * tval) * coef_c * (1.0 + 3.0 * 0.044715 * hval * hval)
    return (activ, deriv)

def reference(inputs, out_grad, pre_act, w_in, w_out):
    scale_value = 1.0 / math.sqrt(TOKENS)
    act_grad = lax.dot_general(out_grad, w_out, (((1,), (1,)), ((), ())), preferred_element_type=jnp.float32)
    activ, deriv = gelu_parts(pre_act)
    activ = activ.astype(jnp.bfloat16)
    hid_grad = (act_grad * deriv).astype(jnp.bfloat16)
    grad_w_out = lax.dot_general(activ, out_grad, (((0,), (0,)), ((), ())), preferred_element_type=jnp.float32)
    grad_w_out = (grad_w_out * scale_value).astype(jnp.bfloat16)
    grad_w_in = lax.dot_general(inputs, hid_grad, (((0,), (0,)), ((), ())), preferred_element_type=jnp.float32)
    grad_w_in = (grad_w_in * scale_value).astype(jnp.bfloat16)
    grad_inputs = lax.dot_general(hid_grad, w_in, (((1,), (1,)), ((), ())), preferred_element_type=jnp.float32)
    return (grad_inputs.astype(jnp.bfloat16), grad_w_in, grad_w_out)
```

```python
import functools
import math

import jax
import jax.numpy as jnp
from jax import lax
from jax.experimental import pallas as pl
from jax.experimental.pallas import tpu as pltpu
from jax.sharding import PartitionSpec as P

coef_c = math.sqrt(2.0 / math.pi)
F32, BF16 = jnp.float32, jnp.bfloat16
MESH = pl.DeviceIdType.MESH

TOK, HID, DM = 768, 768, 1536
NZ, CH, PR = 8, 96, 48
BLK = 24


def gelu_parts(hval):
    tval = jnp.tanh(coef_c * (hval + 0.044715 * hval * hval * hval))
    activ = 0.5 * hval * (1.0 + tval)
    deriv = 0.5 * (1.0 + tval) + 0.5 * hval * (1.0 - tval * tval) * coef_c * (
        1.0 + 3.0 * 0.044715 * hval * hval
    )
    return activ, deriv


def dot_nt(a, b):
    return lax.dot_general(a, b, (((1,), (1,)), ((), ())), preferred_element_type=F32)


def dot_nn(a, b):
    return lax.dot_general(a, b, (((1,), (0,)), ((), ())), preferred_element_type=F32)


def dot_tn(a, b):
    return lax.dot_general(a, b, (((0,), (0,)), ((), ())), preferred_element_type=F32)


def kernel(
    inp_h, og_h, pa_h, win_h, wout_h,
    gi_ref, gwi_h, gwo_h,
    inp, og, pa, win, wout, inpt,
    hid, act, deriv, pbuf,
    rs_s, rs_r,
    gip, pair_r, summed,
    s1, r1, t1, s2, r2,
    gwi, gwo,
    ld_sem, og_sem, st_sem,
    rs_ss, rs_rs, hg_ss, hg_rs, ag_ss, ag_rs, pr_ss, pr_rs,
    x1_ss, x1_rs, x2_ss, x2_rs,
):
    row = lax.axis_index("row")
    z = lax.axis_index("col")
    core = lax.rem(row, 2)
    chip = lax.div(row, 2)
    x = lax.rem(chip, 4)
    y = lax.div(chip, 4)
    scale = 1.0 / math.sqrt(TOK)

    def at(yy, xx, cc):
        return (yy * 4 + xx) * 2 + cc

    def wrap(v, n):
        return lax.rem(v + n, n)

    z_dev = [(row, wrap(z + 1, NZ)), (row, wrap(z - 1, NZ))]
    x_dev = [(at(y, wrap(x + 1, 4), core), z), (at(y, wrap(x - 1, 4), core), z)]
    y_dev = [(at(wrap(y + 1, 4), x, core), z), (at(wrap(y - 1, 4), x, core), z)]
    partner = (at(y, x, 1 - core), z)

    def remote(src, dst, ss, rs, dev):
        return pltpu.make_async_remote_copy(
            src_ref=src, dst_ref=dst, send_sem=ss, recv_sem=rs, device_id=dev, device_id_type=MESH
        )

    def rows(start, size, mult=8):
        return pl.ds(pl.multiple_of(start, mult), size)

    def zc(k):
        return wrap(z + k, NZ)

    def load(src, dst, sem):
        c = pltpu.make_async_copy(src, dst, sem)
        c.start()
        return c

    ld_pa = load(pa_h, pa, ld_sem.at[0])
    order = [4, 3, -3, 2, -2, 1, -1, 0]
    ld_og = {}

    def load_og(n):
        k = order[n]
        ds = rows(zc(k) * CH, CH, 16)
        ld_og[k] = load(og_h.at[ds, :], og.at[ds, :], og_sem.at[n])

    load_og(0)
    ld_wout = load(wout_h, wout, ld_sem.at[1])
    for n in range(1, 8):
        load_og(n)
    ld_win = load(win_h, win, ld_sem.at[2])
    ld_inp = load(inp_h, inp, ld_sem.at[3])

    barrier = pltpu.get_barrier_semaphore()
    peers = z_dev + x_dev + y_dev + [partner]
    for dev in peers:
        pl.semaphore_signal(barrier, inc=1, device_id=dev, device_id_type=MESH)

    ld_pa.wait()
    activ, dv = gelu_parts(pa[...].astype(F32))
    act[rows(z * CH, CH, 16), :] = activ.astype(BF16)
    deriv[...] = dv

    pl.semaphore_wait(barrier, len(peers))

    def ring_piece(buf, ss, rs, d, s, p):
        src_chunk = zc(-s) if d == 0 else zc(s)
        ds = rows(src_chunk * CH + p * PR, PR, 16)
        i = 2 * s + (p if s < 3 else 0)
        return remote(buf.at[ds, :], buf.at[ds, :], ss.at[d, i], rs.at[d, i], z_dev[d])

    def far_piece(d):
        return 0 if d == 0 else 1

    sends = []

    def go(c):
        c.start()
        sends.append(c)
        return c

    ag = {}

    def act_send(d, s, p):
        ag[d, s, p] = go(ring_piece(act, ag_ss, ag_rs, d, s, p))

    for p in range(2):
        for d in range(2):
            act_send(d, 0, p)

    def partial(k, slot):
        ld_og[k].wait()
        a = og[rows(zc(k) * CH, CH, 16), :]
        for n in range(3):
            cs = slice(n * 256, n * 256 + 256)
            pbuf[slot, :, cs] = dot_nt(a, wout[cs, :])

    rs = {}

    def rs_send(d, s, p, value):
        i = 0 if s == 0 else 2 * s - 1 + p
        rs_s[d, i] = value.astype(BF16)
        rs[d, s, p] = go(remote(rs_s.at[d, i], rs_r.at[d, i], rs_ss.at[d, i], rs_rs.at[d, i], z_dev[d]))

    def rs_recv(d, s, p):
        i = 0 if s == 0 else 2 * s - 1 + p
        rs[d, s, p].wait_recv()
        return rs_r[d, i].astype(F32)

    def half(p):
        return slice(p * PR, p * PR + PR)

    ld_wout.wait()
    partial(4, 0)
    for d in range(2):
        p = far_piece(d)
        rs_send(d, 0, p, pbuf[0, half(p), :])
    for s in range(1, 4):
        for d in range(2):
            partial(4 - s if d == 0 else s - 4, d)
            if s == 1:
                p = 1 - far_piece(d)
                rs_send(d, s, p, pbuf[d, half(p), :])
        if s == 1:
            for d in range(2):
                p = far_piece(d)
                rs_send(d, s, p, pbuf[d, half(p), :] + rs_recv(d, 0, p))
        else:
            for q in range(2):
                for d in range(2):
                    p = 1 - far_piece(d) if q == 0 else far_piece(d)
                    rs_send(d, s, p, pbuf[d, half(p), :] + rs_recv(d, s - 1, p))
        if s == 2:
            ld_inp.wait()
        if s >= 2:
            for n in range(3):
                cs = slice((s - 2) * 768 + n * 256, (s - 2) * 768 + n * 256 + 256)
                inpt[cs, :] = inp[:, cs].T

    for d in range(2):
        ag[d, 0, 0].wait_recv()
        act_send(d, 1, 0)

    partial(0, 0)
    hg = {}

    def hid_send(d, s, p):
        hg[d, s, p] = go(ring_piece(hid, hg_ss, hg_rs, d, s, p))

    for p in range(2):
        total = pbuf[0, half(p), :] + rs_recv(0, 3, p) + rs_recv(1, 3, p)
        hid[rows(z * CH + p * PR, PR, 16), :] = (total * deriv[half(p), :]).astype(BF16)
        for d in range(2):
            hid_send(d, 0, p)

    pair = []

    def grad_chunk(k):
        c = zc(k)
        a = hid[rows(c * CH, CH, 16), :]
        for n in range(6):
            cs = slice(n * 256, n * 256 + 256)
            gip[rows(c * CH, CH, 8), cs] = dot_nt(a, win[cs, :])
        i = len(pair) // 2
        for j in range(2):
            src = gip.at[rows(c * CH + (2 * j + 1 - core) * BLK, BLK, 8), :]
            cp = go(remote(src, pair_r.at[i, j], pr_ss.at[i, j], pr_rs.at[i, j], partner))
            pair.append(cp)
        return i

    def pair_sum(k, i):
        c = zc(k)
        for j in range(2):
            pair[2 * i + j].wait_recv()
            own = gip[rows(c * CH + (2 * j + core) * BLK, BLK, 8), :]
            summed[rows((2 * c + j) * BLK, BLK, 8), :] = own + pair_r[i, j]

    ld_win.wait()
    done = [0]
    idx = {0: grad_chunk(0)}
    for s in range(3):
        for p in range(2):
            for d in range(2):
                hg[d, s, p].wait_recv()
                if s < 2 or p == far_piece(d):
                    hid_send(d, s + 1, p)
        if s == 2:
            for d in range(2):
                ag[d, 0, 1].wait_recv()
                act_send(d, 1, 1)
        for k in (-(s + 1), s + 1):
            idx[k] = grad_chunk(k)
        for k in done:
            pair_sum(k, idx[k])
        done = [-(s + 1), s + 1]
    for d in range(2):
        ag[d, 1, 0].wait_recv()
        act_send(d, 2, 0)
    for d in range(2):
        hg[d, 3, far_piece(d)].wait_recv()
    idx[4] = grad_chunk(4)
    for k in done + [4]:
        pair_sum(k, idx[k])
    for d in range(2):
        ag[d, 1, 1].wait_recv()
        act_send(d, 2, 1)

    me = [(x, y), (y, x)]
    devs = [(x_dev, y_dev), (y_dev, x_dev)]

    def own1(h, dest, p):
        if h == 0:
            return jnp.concatenate(
                [summed[rows((q * 4 + dest) * BLK, BLK, 8), :HID] for q in (2 * p, 2 * p + 1)], axis=0
            )
        return summed[rows(dest * 4 * BLK + p * PR, PR, 8), HID:]

    c1, c2 = {}, {}

    def send1(h, d, i, value):
        s1[h, d, i] = value.astype(BF16)
        c1[h, d, i] = go(
            remote(s1.at[h, d, i], r1.at[h, d, i], x1_ss.at[h, d, i], x1_rs.at[h, d, i], devs[h][0][d])
        )

    def recv1(h, d, i):
        c1[h, d, i].wait_recv()
        return r1[h, d, i].astype(F32)

    def own2(h, dest, p):
        return t1[h, rows(dest * BLK, BLK, 8), p * 384 : p * 384 + 384]

    def send2(h, d, i, value):
        s2[h, d, i] = value
        c2[h, d, i] = go(
            remote(s2.at[h, d, i], r2.at[h, d, i], x2_ss.at[h, d, i], x2_rs.at[h, d, i], devs[h][1][d])
        )

    def recv2(h, d, i):
        c2[h, d, i].wait_recv()
        return r2[h, d, i]

    stores = []

    def store(src, dst, i):
        c = pltpu.make_async_copy(src, dst, st_sem.at[i])
        c.start()
        stores.append(c)

    def grad_w_in_tile(i):
        rs_ = slice(i * 256, i * 256 + 256)
        gwi[rs_, :] = (dot_nn(inpt[rs_, :], hid[...]) * scale).astype(BF16)
        store(gwi.at[rs_, :], gwi_h.at[rs_, :], i)

    def grad_w_out_tile(i):
        rs_ = slice(i * 256, i * 256 + 256)
        gwo[rs_, :] = (dot_tn(act[:, rs_], og[...]) * scale).astype(BF16)
        store(gwo.at[rs_, :], gwo_h.at[rs_, :], 6 + i)

    step = (1, -1)
    for h in range(2):
        for d in range(2):
            send1(h, d, 0, own1(h, wrap(me[h][0] + 2, 4), far_piece(d)))
    for h in range(2):
        for d in range(2):
            send1(h, d, 1, own1(h, wrap(me[h][0] + step[d], 4), 1 - far_piece(d)))
    grad_w_in_tile(0)
    grad_w_in_tile(1)
    for h in range(2):
        for d in range(2):
            p = far_piece(d)
            send1(h, d, 2, own1(h, wrap(me[h][0] + step[d], 4), p) + recv1(h, d, 0))
    for d in range(2):
        p = far_piece(d)
        ag[d, 2, p].wait_recv()
        act_send(d, 3, p)
    grad_w_in_tile(2)
    grad_w_in_tile(3)
    for h in range(2):
        for p in range(2):
            fwd = recv1(h, 0, 2 if p == 0 else 1)
            bwd = recv1(h, 1, 1 if p == 0 else 2)
            t1[h, half(p), :] = own1(h, me[h][0], p) + fwd + bwd
    for h in range(2):
        for d in range(2):
            send2(h, d, 0, own2(h, wrap(me[h][1] + 2, 4), far_piece(d)))
    for h in range(2):
        for d in range(2):
            send2(h, d, 1, own2(h, wrap(me[h][1] + step[d], 4), 1 - far_piece(d)))
    grad_w_in_tile(4)
    grad_w_in_tile(5)
    for h in range(2):
        for d in range(2):
            p = far_piece(d)
            send2(h, d, 2, own2(h, wrap(me[h][1] + step[d], 4), p) + recv2(h, d, 0))
    for d in range(2):
        ag[d, 2, 1 - far_piece(d)].wait_recv()
        ag[d, 3, far_piece(d)].wait_recv()
    for i in range(3):
        grad_w_out_tile(i)
    for h in range(2):
        for p in range(2):
            fwd = recv2(h, 0, 2 if p == 0 else 1)
            bwd = recv2(h, 1, 1 if p == 0 else 2)
            c0 = h * HID + p * 384
            gi_ref[:, c0 : c0 + 384] = (own2(h, me[h][1], p) + fwd + bwd).astype(BF16)

    for c in sends:
        c.wait_send()
    for c in stores:
        c.wait()


def per_device(inputs, out_grad, pre_act, w_in, w_out):
    any_spec = pl.BlockSpec(memory_space=pl.ANY)
    vm = pltpu.VMEM
    dma = pltpu.SemaphoreType.DMA
    return pl.pallas_call(
        kernel,
        out_shape=(
            jax.ShapeDtypeStruct((BLK, DM), BF16),
            jax.ShapeDtypeStruct((DM, HID), BF16),
            jax.ShapeDtypeStruct((HID, DM), BF16),
        ),
        in_specs=[any_spec] * 5,
        out_specs=(pl.BlockSpec(memory_space=pltpu.VMEM), any_spec, any_spec),
        scratch_shapes=[
            vm((TOK, DM), BF16), vm((TOK, DM), BF16), vm((CH, HID), BF16),
            vm((DM, HID), BF16), vm((HID, DM), BF16), vm((DM, TOK), BF16),
            vm((TOK, HID), BF16), vm((TOK, HID), BF16), vm((CH, HID), F32), vm((2, CH, HID), F32),
            vm((2, 7, PR, HID), BF16), vm((2, 7, PR, HID), BF16),
            vm((TOK, DM), F32), vm((8, 2, BLK, DM), F32), vm((TOK // 2, DM), F32),
            vm((2, 2, 3, PR, HID), BF16), vm((2, 2, 3, PR, HID), BF16), vm((2, CH, HID), F32),
            vm((2, 2, 3, BLK, 384), F32), vm((2, 2, 3, BLK, 384), F32),
            vm((DM, HID), BF16), vm((HID, DM), BF16),
            dma((4,)), dma((8,)), dma((9,)),
            dma((2, 7)), dma((2, 7)), dma((2, 7)), dma((2, 7)), dma((2, 7)), dma((2, 7)),
            dma((8, 2)), dma((8, 2)),
            dma((2, 2, 3)), dma((2, 2, 3)), dma((2, 2, 3)), dma((2, 2, 3)),
        ],
        compiler_params=pltpu.CompilerParams(
            collective_id=0, has_side_effects=True, vmem_limit_bytes=60 * 1024 * 1024
        ),
        name="ffn_backward",
    )(inputs, out_grad, pre_act, w_in, w_out)


def solution(mesh):
    placed = (P(None, "col"), P(None, "col"), P("col", "row"), P("col", "row"), P("row", "col"))
    return jax.shard_map(
        per_device,
        mesh=mesh,
        in_specs=placed,
        out_specs=(P("row", "col"), P("col", "row"), P("row", "col")),
        check_vma=False,
    )
```

```python
import functools
import math

import jax
import jax.numpy as jnp
from jax import lax
from jax.experimental import pallas as pl
from jax.experimental.pallas import tpu as pltpu
from jax.sharding import PartitionSpec as P

coef_c = math.sqrt(2.0 / math.pi)
F32, BF16 = jnp.float32, jnp.bfloat16
MESH = pl.DeviceIdType.MESH

TOK, HID, DM = 768, 768, 1536
NZ, CH, PR = 8, 96, 48
PC = 384
BLK = 24


def gelu_parts(hval):
    tval = jnp.tanh(coef_c * (hval + 0.044715 * hval * hval * hval))
    activ = 0.5 * hval * (1.0 + tval)
    deriv = 0.5 * (1.0 + tval) + 0.5 * hval * (1.0 - tval * tval) * coef_c * (
        1.0 + 3.0 * 0.044715 * hval * hval
    )
    return activ, deriv


def dot_nt(a, b):
    return lax.dot_general(a, b, (((1,), (1,)), ((), ())), preferred_element_type=F32)


def dot_nn(a, b):
    return lax.dot_general(a, b, (((1,), (0,)), ((), ())), preferred_element_type=F32)


def dot_tn(a, b):
    return lax.dot_general(a, b, (((0,), (0,)), ((), ())), preferred_element_type=F32)


def kernel(
    inp_h, og_h, pa_h, win_h, wout_h,
    gi_ref, gwi_h, gwo_h,
    inp, og, pa, win, wout, inpt,
    hid, act, deriv, pbuf,
    rs_s, rs_r,
    gip, pair_r, summed,
    s1, r1, t1, s2, r2,
    gwi, gwo,
    ld_sem, og_sem, st_sem,
    rs_ss, rs_rs, hg_ss, hg_rs, ag_ss, ag_rs, pr_ss, pr_rs,
    x1_ss, x1_rs, x2_ss, x2_rs,
):
    row = lax.axis_index("row")
    z = lax.axis_index("col")
    core = lax.rem(row, 2)
    chip = lax.div(row, 2)
    x = lax.rem(chip, 4)
    y = lax.div(chip, 4)
    scale = 1.0 / math.sqrt(TOK)

    def at(yy, xx, cc):
        return (yy * 4 + xx) * 2 + cc

    def wrap(v, n):
        return lax.rem(v + n, n)

    z_dev = [(row, wrap(z + 1, NZ)), (row, wrap(z - 1, NZ))]
    x_dev = [(at(y, wrap(x + 1, 4), core), z), (at(y, wrap(x - 1, 4), core), z)]
    y_dev = [(at(wrap(y + 1, 4), x, core), z), (at(wrap(y - 1, 4), x, core), z)]
    partner = (at(y, x, 1 - core), z)

    def remote(src, dst, ss, rs, dev):
        return pltpu.make_async_remote_copy(
            src_ref=src, dst_ref=dst, send_sem=ss, recv_sem=rs, device_id=dev, device_id_type=MESH
        )

    def rows(start, size, mult=8):
        return pl.ds(pl.multiple_of(start, mult), size)

    def zc(k):
        return wrap(z + k, NZ)

    def load(src, dst, sem):
        c = pltpu.make_async_copy(src, dst, sem)
        c.start()
        return c

    ld_pa = load(pa_h, pa, ld_sem.at[0])
    order = [4, 3, -3, 2, -2, 1, -1, 0]
    ld_og = {}

    def load_og(n):
        k = order[n]
        ds = rows(zc(k) * CH, CH, 16)
        ld_og[k] = load(og_h.at[ds, :], og.at[ds, :], og_sem.at[n])

    load_og(0)
    ld_wout = load(wout_h, wout, ld_sem.at[1])
    for n in range(1, 8):
        load_og(n)
    ld_win = load(win_h, win, ld_sem.at[2])
    ld_inp = load(inp_h, inp, ld_sem.at[3])

    barrier = pltpu.get_barrier_semaphore()
    peers = z_dev + x_dev + y_dev + [partner]
    for dev in peers:
        pl.semaphore_signal(barrier, inc=1, device_id=dev, device_id_type=MESH)

    ld_pa.wait()
    activ, dv = gelu_parts(pa[...].astype(F32))
    act[rows(z * CH, CH, 16), :] = activ.astype(BF16)
    deriv[...] = dv

    sends = []

    def go(c):
        c.start()
        sends.append(c)
        return c

    def far_piece(d):
        return 0 if d == 0 else 1

    def chunk_at(d, s):
        return zc(-s) if d == 0 else zc(s)

    ag = {}

    def act_send(d, s, p):
        ds = rows(chunk_at(d, s) * CH + p * PR, PR, 16)
        i = 2 * s + (p if s < 3 else 0)
        ag[d, s, p] = go(remote(act.at[ds, :], act.at[ds, :], ag_ss.at[d, i], ag_rs.at[d, i], z_dev[d]))

    def partial(k):
        ld_og[k].wait()
        a = og[rows(zc(k) * CH, CH, 16), :]
        for n in range(3):
            cs = slice(n * 256, n * 256 + 256)
            pbuf[k + 3, :, cs] = dot_nt(a, wout[cs, :])

    pieces = [(0, 0), (1, 0), (0, 1), (1, 1)]

    def piece_id(s, q):
        return q[1] if s == 0 else 4 * s - 2 + 2 * q[0] + q[1]

    def fwd_id(s, q):
        return 4 * s + (2 * q[0] + q[1] if s < 3 else q[1])

    def part(q):
        return slice(q[0] * PR, q[0] * PR + PR), slice(q[1] * PC, q[1] * PC + PC)

    rs = {}

    def rs_send(d, s, q):
        i = piece_id(s, q)
        r, c = part(q)
        value = pbuf[(4 - s if d == 0 else (s - 4 if s else 4)) + 3, r, c]
        if (d, s - 1, q) in rs:
            value = value + rs_recv(d, s - 1, q)
        rs_s[d, i] = value.astype(BF16)
        rs[d, s, q] = go(remote(rs_s.at[d, i], rs_r.at[d, i], rs_ss.at[d, i], rs_rs.at[d, i], z_dev[d]))

    def rs_recv(d, s, q):
        rs[d, s, q].wait_recv()
        return rs_r[d, piece_id(s, q)].astype(F32)

    def half(p):
        return slice(p * PR, p * PR + PR)

    def transpose(n):
        cs = slice(n * 256, n * 256 + 256)
        inpt[cs, :] = inp[:, cs].T

    ld_wout.wait()
    partial(4)
    partial(3)
    partial(-3)
    pl.semaphore_wait(barrier, len(peers))
    for c in range(2):
        for d in range(2):
            rs_send(d, 0, (far_piece(d), c))
    for c in range(2):
        for d in range(2):
            rs_send(d, 1, (1 - far_piece(d), c))
    partial(2)
    partial(-2)
    for c in range(2):
        for d in range(2):
            rs_send(d, 1, (far_piece(d), c))
    partial(1)
    partial(-1)
    for s in (2, 3):
        for far in range(2):
            for c in range(2):
                for d in range(2):
                    rs_send(d, s, (far_piece(d) if far else 1 - far_piece(d), c))
            if s == 2 and far == 0:
                partial(0)
            if s == 2 and far == 1:
                ld_inp.wait()
                for n in range(3):
                    transpose(n)
            if s == 3 and far == 0:
                for n in range(3, 6):
                    transpose(n)

    for d in range(2):
        act_send(d, 0, 0)

    hg = {}

    def hid_send(d, s, q):
        ds = rows(chunk_at(d, s) * CH + q[0] * PR, PR, 16)
        src = hid.at[ds, q[1] * PC : q[1] * PC + PC]
        i = fwd_id(s, q)
        hg[d, s, q] = go(remote(src, src, hg_ss.at[d, i], hg_rs.at[d, i], z_dev[d]))

    for q in pieces:
        r, c = part(q)
        total = pbuf[3, r, c] + rs_recv(0, 3, q) + rs_recv(1, 3, q)
        hid[rows(z * CH + q[0] * PR, PR, 16), c] = (total * deriv[r, c]).astype(BF16)
        for d in range(2):
            hid_send(d, 0, q)

    pair = {}

    def grad_half(k, m):
        c = zc(k)
        a = hid[rows(c * CH, CH, 16), :]
        for n in range(3 * m, 3 * m + 3):
            cs = slice(n * 256, n * 256 + 256)
            gip[rows(c * CH, CH, 8), cs] = dot_nt(a, win[cs, :])
        if m == 1:
            for j in range(2):
                i = k + 3
                src = gip.at[rows(c * CH + (2 * j + 1 - core) * BLK, BLK, 8), :]
                pair[k, j] = go(remote(src, pair_r.at[i, j], pr_ss.at[i, j], pr_rs.at[i, j], partner))

    def pair_sum(k):
        c = zc(k)
        for j in range(2):
            pair[k, j].wait_recv()
            own = gip[rows(c * CH + (2 * j + core) * BLK, BLK, 8), :]
            summed[rows((2 * c + j) * BLK, BLK, 8), :] = own + pair_r[k + 3, j]

    ld_win.wait()
    work = [(grad_half, 0, 0), (grad_half, 0, 1)]

    def tick():
        if work:
            item = work.pop(0)
            item[0](*item[1:])

    last = [0]
    for s in range(3):
        for q in pieces:
            for d in range(2):
                hg[d, s, q].wait_recv()
                if s < 2 or q[0] == far_piece(d):
                    hid_send(d, s + 1, q)
            tick()
        while work:
            tick()
        for k in last:
            work.append((pair_sum, k))
        last = [-(s + 1), s + 1]
        for k in last:
            work += [(grad_half, k, 0), (grad_half, k, 1)]
        work.sort(key=lambda w: w[0] is pair_sum)
    for d in range(2):
        act_send(d, 0, 1)
        ag[d, 0, 0].wait_recv()
        act_send(d, 1, 0)
    while work:
        tick()
    for c in range(2):
        for d in range(2):
            hg[d, 3, (far_piece(d), c)].wait_recv()
    grad_half(4, 0)
    grad_half(4, 1)
    for d in range(2):
        ag[d, 0, 1].wait_recv()
        act_send(d, 1, 1)
    for k in last + [4]:
        pair_sum(k)

    me = [(x, y), (y, x)]
    devs = [(x_dev, y_dev), (y_dev, x_dev)]

    def own1(h, dest, p):
        if h == 0:
            return jnp.concatenate(
                [summed[rows((q * 4 + dest) * BLK, BLK, 8), :HID] for q in (2 * p, 2 * p + 1)], axis=0
            )
        return summed[rows(dest * 4 * BLK + p * PR, PR, 8), HID:]

    c1, c2 = {}, {}

    def send1(h, d, i, value):
        s1[h, d, i] = value.astype(BF16)
        c1[h, d, i] = go(
            remote(s1.at[h, d, i], r1.at[h, d, i], x1_ss.at[h, d, i], x1_rs.at[h, d, i], devs[h][0][d])
        )

    def recv1(h, d, i):
        c1[h, d, i].wait_recv()
        return r1[h, d, i].astype(F32)

    def own2(h, dest, p):
        return t1[h, rows(dest * BLK, BLK, 8), p * 384 : p * 384 + 384]

    def send2(h, d, i, value):
        s2[h, d, i] = value
        c2[h, d, i] = go(
            remote(s2.at[h, d, i], r2.at[h, d, i], x2_ss.at[h, d, i], x2_rs.at[h, d, i], devs[h][1][d])
        )

    def recv2(h, d, i):
        c2[h, d, i].wait_recv()
        return r2[h, d, i]

    stores = []

    def store(src, dst, i):
        c = pltpu.make_async_copy(src, dst, st_sem.at[i])
        c.start()
        stores.append(c)

    def grad_w_in_tile(i):
        rs_ = slice(i * 256, i * 256 + 256)
        gwi[rs_, :] = (dot_nn(inpt[rs_, :], hid[...]) * scale).astype(BF16)
        store(gwi.at[rs_, :], gwi_h.at[rs_, :], i)

    def grad_w_out_tile(i):
        rs_ = slice(i * 256, i * 256 + 256)
        gwo[rs_, :] = (dot_tn(act[:, rs_], og[...]) * scale).astype(BF16)
        store(gwo.at[rs_, :], gwo_h.at[rs_, :], 6 + i)

    step = (1, -1)
    for h in range(2):
        for d in range(2):
            send1(h, d, 0, own1(h, wrap(me[h][0] + 2, 4), far_piece(d)))
    for h in range(2):
        for d in range(2):
            send1(h, d, 1, own1(h, wrap(me[h][0] + step[d], 4), 1 - far_piece(d)))
    for d in range(2):
        ag[d, 1, 0].wait_recv()
        act_send(d, 2, 0)
    grad_w_in_tile(0)
    grad_w_in_tile(1)
    for h in range(2):
        for d in range(2):
            p = far_piece(d)
            send1(h, d, 2, own1(h, wrap(me[h][0] + step[d], 4), p) + recv1(h, d, 0))
    for d in range(2):
        ag[d, 1, 1].wait_recv()
        act_send(d, 2, 1)
    grad_w_in_tile(2)
    grad_w_in_tile(3)
    for h in range(2):
        for p in range(2):
            fwd = recv1(h, 0, 2 if p == 0 else 1)
            bwd = recv1(h, 1, 1 if p == 0 else 2)
            t1[h, half(p), :] = own1(h, me[h][0], p) + fwd + bwd
    for h in range(2):
        for d in range(2):
            send2(h, d, 0, own2(h, wrap(me[h][1] + 2, 4), far_piece(d)))
    for h in range(2):
        for d in range(2):
            send2(h, d, 1, own2(h, wrap(me[h][1] + step[d], 4), 1 - far_piece(d)))
    grad_w_in_tile(4)
    grad_w_in_tile(5)
    for d in range(2):
        p = far_piece(d)
        ag[d, 2, p].wait_recv()
        act_send(d, 3, p)
    for h in range(2):
        for d in range(2):
            p = far_piece(d)
            send2(h, d, 2, own2(h, wrap(me[h][1] + step[d], 4), p) + recv2(h, d, 0))
    for d in range(2):
        ag[d, 2, 1 - far_piece(d)].wait_recv()
        ag[d, 3, far_piece(d)].wait_recv()
    for i in range(3):
        grad_w_out_tile(i)
    for h in range(2):
        for p in range(2):
            fwd = recv2(h, 0, 2 if p == 0 else 1)
            bwd = recv2(h, 1, 1 if p == 0 else 2)
            c0 = h * HID + p * 384
            gi_ref[:, c0 : c0 + 384] = (own2(h, me[h][1], p) + fwd + bwd).astype(BF16)

    for c in sends:
        c.wait_send()
    for c in stores:
        c.wait()


def finish(gi_t, gwi_t, gwo_t, gi, gwi, gwo, gi_v, gwi_v, gwo_v, in_sem, out_sem):
    jobs = [(gi_t, gi_v, gi)]
    for n in range(3):
        for t, v, o in ((gwi_t, gwi_v, gwi), (gwo_t, gwo_v, gwo)):
            size = t.shape[0] // 3
            ds = slice(n * size, n * size + size)
            jobs.append((t.at[ds, :], v.at[ds, :], o.at[ds, :]))
    ins = [pltpu.make_async_copy(t, v, in_sem.at[i]) for i, (t, v, o) in enumerate(jobs)]
    outs = [pltpu.make_async_copy(v, o, out_sem.at[i]) for i, (t, v, o) in enumerate(jobs)]
    for c in ins:
        c.start()
    for c, o in zip(ins, outs):
        c.wait()
        o.start()
    for o in outs:
        o.wait()


def per_device(inputs, out_grad, pre_act, w_in, w_out):
    any_spec = pl.BlockSpec(memory_space=pl.ANY)
    vm = pltpu.VMEM
    dma = pltpu.SemaphoreType.DMA
    shapes = (
        jax.ShapeDtypeStruct((BLK, DM), BF16),
        jax.ShapeDtypeStruct((DM, HID), BF16),
        jax.ShapeDtypeStruct((HID, DM), BF16),
    )
    results = pl.pallas_call(
        kernel,
        out_shape=shapes,
        in_specs=[any_spec] * 5,
        out_specs=(pl.BlockSpec(memory_space=pltpu.VMEM), any_spec, any_spec),
        scratch_shapes=[
            vm((TOK, DM), BF16), vm((TOK, DM), BF16), vm((CH, HID), BF16),
            vm((DM, HID), BF16), vm((HID, DM), BF16), vm((DM, TOK), BF16),
            vm((TOK, HID), BF16), vm((TOK, HID), BF16), vm((CH, HID), F32), vm((8, CH, HID), F32),
            vm((2, 14, PR, PC), BF16), vm((2, 14, PR, PC), BF16),
            vm((TOK, DM), F32), vm((8, 2, BLK, DM), F32), vm((TOK // 2, DM), F32),
            vm((2, 2, 3, PR, HID), BF16), vm((2, 2, 3, PR, HID), BF16), vm((2, CH, HID), F32),
            vm((2, 2, 3, BLK, 384), F32), vm((2, 2, 3, BLK, 384), F32),
            vm((DM, HID), BF16), vm((HID, DM), BF16),
            dma((4,)), dma((8,)), dma((9,)),
            dma((2, 14)), dma((2, 14)), dma((2, 14)), dma((2, 14)), dma((2, 7)), dma((2, 7)),
            dma((8, 2)), dma((8, 2)),
            dma((2, 2, 3)), dma((2, 2, 3)), dma((2, 2, 3)), dma((2, 2, 3)),
        ],
        compiler_params=pltpu.CompilerParams(
            collective_id=0, has_side_effects=True, vmem_limit_bytes=60 * 1024 * 1024
        ),
        name="ffn_backward",
    )(inputs, out_grad, pre_act, w_in, w_out)
    return pl.pallas_call(
        finish,
        out_shape=shapes,
        in_specs=[any_spec] * 3,
        out_specs=(any_spec,) * 3,
        scratch_shapes=[
            vm((BLK, DM), BF16), vm((DM, HID), BF16), vm((HID, DM), BF16), dma((7,)), dma((7,)),
        ],
        name="finish",
    )(*results)


def solution(mesh):
    placed = (P(None, "col"), P(None, "col"), P("col", "row"), P("col", "row"), P("row", "col"))
    return jax.shard_map(
        per_device,
        mesh=mesh,
        in_specs=placed,
        out_specs=(P("row", "col"), P("col", "row"), P("row", "col")),
        check_vma=False,
    )
```
